32 devices in a mesh: kgrp: 4 (over x, core), band: 8 (over z, y).
Axes of the slice: x: 2, y: 2, z: 4, core: 2. Of those that a mesh axis runs over, the one named last changes fastest.
Arguments:
- densities: bfloat16 [8, 128, 128, 4096], P('kgrp', 'band'), may hold values from -6 to 6
- amplitudes: bfloat16 [8, 8, 128, 128], P('kgrp'), may hold values from -0.046875 to 0.046875
- partner: int32 [8], replicated, may hold values from 0 to 7, as said below
- qtable: int32 [8], replicated, may hold values from 0 to 63
- grid_map: int32 [64, 4096], replicated, may hold values from 0 to 4095, each once within a row
- coulomb: float32 [64, 4096], replicated, may hold values from 0.5 to 2
Outputs:
- ladder: bfloat16 [128, 8, 8, 128], P('band', 'kgrp')
The draws below stay inside these ranges and needn't reach their ends.
Inputs may be any that keep to these rules, and one draw needn't show every extreme that they name: partner is a permutation of the 8 k-pairs; k-pair r lies in group r // 2. The two pairs of a group have their partners in two different groups, neither of them the group itself, and the two pairs whose partners lie in one group belong to two different groups. `grid_map`: each row is a permutation of the 4096 grid positions.
All inputs are finite; a program needn't handle non-finite values.
Results may differ from the reference program's by a relative error of at most 0.0064.
Values may be sent and summed in bfloat16 or wider, within the bound.
A program may use at most 448 MiB of HBM per device.

```python
import math
import jax
import jax.numpy as jnp
from jax import lax

VB = 128
G = 4096
NQ = 64
IJ = 8
NK = 8


def draw_partner(key, part):
    groups = NK // 2
    first_shift = jax.random.randint(jax.random.fold_in(key, 21), (), 1, groups)
    offset = jax.random.randint(jax.random.fold_in(key, 22), (), 0, groups - 2)
    second_shift = (first_shift + offset) % (groups - 1) + 1
    sender_bit = jax.random.randint(jax.random.fold_in(key, 23), (groups,), 0, 2)
    receiver_bit = jax.random.randint(jax.random.fold_in(key, 24), (groups,), 0, 2)
    group_ids = jnp.arange(groups, dtype=jnp.int32)
    first_dest = (group_ids + first_shift) % groups
    second_dest = (group_ids + second_shift) % groups
    first_target = 2 * first_dest + receiver_bit[first_dest]
    second_target = 2 * second_dest + 1 - receiver_bit[second_dest]
    slot_zero = jnp.where(sender_bit == 0, first_target, second_target)
    slot_one = jnp.where(sender_bit == 0, second_target, first_target)
    return jnp.stack([slot_zero, slot_one], axis=1).reshape(NK).astype(jnp.int32)


def with_ends(entries, key, low, largest):
    place = [jax.random.randint(jax.random.fold_in(key, axis), (), 0, length) for axis, length in enumerate(entries.shape)]
    main_axis = entries.shape.index(max(entries.shape))
    beside = place[:main_axis] + [(place[main_axis] + 1) % entries.shape[main_axis]] + place[main_axis + 1:]
    return entries.at[tuple(place)].set(low).at[tuple(beside)].set(largest)


def spiked(entries, own_key, source, target, blocks, factor):
    owner, partner = [(jnp.arange(entries.shape[axis_at]) // (entries.shape[axis_at] // blocks)).reshape([-1 if axis == axis_at else 1 for axis in range(entries.ndim)]) for axis_at in (source, target)]
    chosen = jax.random.permutation(own_key, blocks)[partner]
    strong = (owner == chosen) | (owner == (partner + blocks // 2) % blocks)
    return jnp.where(strong, factor * entries, entries)


def block_levels(stream_key, extent, shards, least, top_value):
    def one(axis_at, blocks):
        draws = jax.random.uniform(jax.random.fold_in(jax.random.fold_in(stream_key, 6), axis_at), (blocks,), jnp.float32, least / len(shards), top_value / len(shards))
        return jnp.repeat(jnp.exp(draws), extent[axis_at] // blocks).reshape((-1,) + (1,) * (len(extent) - axis_at - 1))

    gain = one(*shards[0])
    for cut in shards[1:]:
        gain = gain * one(*cut)
    return gain


def normal_values(stream_key, shape, spread, bound, shards=(), kind=jnp.bfloat16):
    loudness = block_levels(stream_key, shape, shards, -0.22, 0.18) if shards else 1.0
    drawn = jax.random.normal(stream_key, shape, jnp.float32) * spread * loudness
    return jnp.minimum(jnp.maximum(drawn, -bound), bound).astype(kind)


def bell_draw_with(stream_key, extent, scale, reach, cuts, heavy, held_as=jnp.bfloat16):
    array = scale * jax.random.normal(stream_key, extent, jnp.float32)
    if cuts:
        array = array * block_levels(stream_key, extent, cuts, -0.22, 0.18)
    return jnp.clip(spiked(array, jax.random.fold_in(stream_key, 3), *heavy), -reach, reach).astype(held_as)


def setup_inputs(seed: int = 0) -> dict:
    arg_keys = jax.random.split(jax.random.key(seed), 7)
    return {
        "densities": bell_draw_with(arg_keys[0], (NK, VB, VB, G), 1.0, 6.0, ((0, 4), (1, 8)), (3, 1, 8, 2.0)),
        "amplitudes": normal_values(arg_keys[1], (NK, IJ, VB, VB), (VB * VB) ** -0.5, 0.046875, ((0, 4),)),
        "partner": draw_partner(jax.random.fold_in(arg_keys[6], 71), 0),
        "qtable": with_ends(jax.random.randint(arg_keys[3], (NK,), 0, NQ), jax.random.fold_in(arg_keys[3], 1), 0, NQ - 1).astype(jnp.int32),
        "grid_map": jax.vmap(lambda own: jax.random.permutation(own, G))(jax.random.split(arg_keys[4], NQ)).reshape((NQ, G)).astype(jnp.int32),
        "coulomb": jnp.clip(jnp.exp(jax.random.uniform(arg_keys[5], (NQ, G), jnp.float32, math.log(0.5), math.log(2.0))), 0.5, 2.0),
    }


def make_vertex(densities, qtable, grid_map, coulomb, pair_index):
    transfer = qtable[pair_index]
    grid_rows = grid_map[transfer]
    factors = coulomb[transfer]
    picked = jnp.take(densities[pair_index], grid_rows, axis=2)
    return (picked.astype(jnp.float32) * factors[None, None, :]).astype(jnp.bfloat16)

def reference(densities, amplitudes, partner, qtable, grid_map, coulomb):

    def per_pair(pair_index):
        left_block = make_vertex(densities, qtable, grid_map, coulomb, pair_index)
        right_block = make_vertex(densities, qtable, grid_map, coulomb, partner[pair_index])
        left_wide = left_block.astype(jnp.float32)
        right_wide = right_block.astype(jnp.float32)

        def per_slab(amp_pair):
            mixed = jnp.einsum('acg,cd->adg', left_wide, amp_pair.astype(jnp.float32)).astype(jnp.bfloat16)
            return jnp.einsum('adg,bdg->ab', mixed.astype(jnp.float32), right_wide)
        return lax.map(per_slab, amplitudes[pair_index])
    sums = lax.map(per_pair, jnp.arange(NK, dtype=jnp.int32))
    scaled = sums * (1.0 / math.sqrt(G))
    return jnp.transpose(scaled, (2, 0, 1, 3)).astype(jnp.bfloat16)
```

```python
import functools
import math

import jax
import jax.numpy as jnp
from jax import lax
from jax.experimental import pallas as pl
from jax.experimental.pallas import tpu as pltpu
from jax.sharding import PartitionSpec as P


def ladder_kernel(partner_ref, left_ref, right_ref, amp_ref, out_ref):
    step = pl.program_id(1)
    bands, depth, rows, width = left_ref.shape[2:]
    vb = bands * rows
    slabs = amp_ref.shape[2] // width
    left = jnp.concatenate([left_ref[0, 0, :, g].reshape(vb, width) for g in range(depth)], axis=0)
    right = jnp.concatenate([right_ref[0, 0, :, g].reshape(vb, width) for g in range(depth)], axis=1)
    mixed = jnp.dot(left, amp_ref[0], preferred_element_type=jnp.float32).astype(jnp.bfloat16)
    wide = jnp.concatenate(
        [
            jnp.concatenate(
                [mixed[g * vb:(g + 1) * vb, s * width:(s + 1) * width] for g in range(depth)], axis=1
            )
            for s in range(slabs)
        ],
        axis=0,
    )
    part = lax.dot_general(wide, right, (((1,), (1,)), ((), ())), preferred_element_type=jnp.float32)

    @pl.when(step == 0)
    def _():
        out_ref[0] = part

    @pl.when(step > 0)
    def _():
        out_ref[0] += part


def ladder_sums(blocks, amps, partner, depth):
    per_group, groups, bands, g_shard, rows, width = blocks.shape
    pairs = per_group * groups
    vb = bands * rows
    slabs = amps.shape[2] // width

    def left_map(r, s, partner_ref):
        return (lax.rem(r, per_group), r // per_group, 0, s, 0, 0)

    def right_map(r, s, partner_ref):
        q = partner_ref[r]
        return (lax.rem(q, per_group), q // per_group, 0, s, 0, 0)

    spec = (1, 1, bands, depth, rows, width)
    return pl.pallas_call(
        ladder_kernel,
        grid_spec=pltpu.PrefetchScalarGridSpec(
            num_scalar_prefetch=1,
            grid=(pairs, g_shard // depth),
            in_specs=[
                pl.BlockSpec(spec, left_map),
                pl.BlockSpec(spec, right_map),
                pl.BlockSpec((1,) + amps.shape[1:], lambda r, s, p: (r, 0, 0)),
            ],
            out_specs=pl.BlockSpec((1, slabs * vb, vb), lambda r, s, p: (r, 0, 0)),
        ),
        out_shape=jax.ShapeDtypeStruct((pairs, slabs * vb, vb), jnp.float32),
        name="ladder",
    )(partner, blocks, blocks, amps)


def shards(group_count, band_count, densities, amplitudes, partner, qtable, grid_map, coulomb):
    my_group = lax.axis_index("kgrp")
    per_group, rows, width, g_all = densities.shape
    slabs = amplitudes.shape[1]
    vb = rows * band_count
    devices = group_count * band_count
    own_ids = my_group * per_group + jnp.arange(per_group, dtype=jnp.int32)
    transfers = jnp.take(qtable, own_ids)
    positions = jnp.take(grid_map, transfers, axis=0)
    factors = jnp.take(coulomb, transfers, axis=0)
    turned = jnp.transpose(densities, (0, 3, 1, 2))
    picked = jax.vmap(lambda block, index: jnp.take(block, index, axis=0))(turned, positions)
    vertex = (picked.astype(jnp.float32) * factors[:, :, None, None]).astype(jnp.bfloat16)
    g_shard = g_all // devices
    vertex = vertex.reshape(per_group, devices, g_shard, rows, width)
    moved = lax.all_to_all(vertex, ("kgrp", "band"), split_axis=1, concat_axis=1, tiled=True)
    blocks = moved.reshape(per_group, group_count, band_count, g_shard, rows, width)
    amps = lax.all_gather(amplitudes, "kgrp", axis=0, tiled=True)
    amps = jnp.transpose(amps, (0, 2, 1, 3)).reshape(-1, width, slabs * width)
    sums = ladder_sums(blocks, amps, partner, math.gcd(g_shard, 8))
    sums = sums.reshape(-1, slabs, vb, vb)
    sums = lax.psum_scatter(sums, "kgrp", scatter_dimension=0, tiled=True)
    sums = lax.psum_scatter(sums, "band", scatter_dimension=2, tiled=True)
    scaled = sums * (1.0 / math.sqrt(g_all))
    return jnp.transpose(scaled, (2, 0, 1, 3)).astype(jnp.bfloat16)


def solution(mesh):
    in_specs = (P("kgrp", "band", None, None), P("kgrp", None, None, None), P(), P(), P(), P())
    out_specs = P("band", "kgrp", None, None)
    body = functools.partial(shards, mesh.shape["kgrp"], mesh.shape["band"])
    return jax.shard_map(body, mesh=mesh, in_specs=in_specs, out_specs=out_specs, check_vma=False)
```

```python
import functools
import math

import jax
import jax.numpy as jnp
from jax import lax
from jax.experimental import pallas as pl
from jax.experimental.pallas import tpu as pltpu
from jax.sharding import PartitionSpec as P

CUTS = (1, 3, 3, 1)


def pick_kernel(index_ref, factor_ref, source_ref, out_ref):
    pair = pl.program_id(0)
    devices, _, depth = out_ref.shape[:3]

    def one(i, carry):
        d, g = i // depth, lax.rem(i, depth)
        row = source_ref[0, index_ref[pair, i]].astype(jnp.float32) * factor_ref[pair, i]
        out_ref[d, 0, g] = row.astype(out_ref.dtype)
        return carry

    lax.fori_loop(0, devices * depth, one, 0, unroll=8)


def pick_rows(turned, index, factors):
    pairs, g_all, rows, width = turned.shape
    devices, depth = index.shape[1:]
    return pl.pallas_call(
        pick_kernel,
        grid_spec=pltpu.PrefetchScalarGridSpec(
            num_scalar_prefetch=2,
            grid=(pairs,),
            in_specs=[pl.BlockSpec((1, g_all, rows, width), lambda p, i, f: (p, 0, 0, 0))],
            out_specs=pl.BlockSpec((devices, 1, depth, rows, width), lambda p, i, f: (0, p, 0, 0, 0)),
        ),
        out_shape=jax.ShapeDtypeStruct((devices, pairs, depth, rows, width), turned.dtype),
        cost_estimate=pl.CostEstimate(
            flops=pairs * devices * depth * rows * width,
            bytes_accessed=2 * turned.size + 2 * pairs * devices * depth * rows * width,
            transcendentals=0,
        ),
        compiler_params=pltpu.CompilerParams(vmem_limit_bytes=62 * 1024 * 1024),
        name="pick_rows",
    )(index.reshape(pairs, -1), factors.reshape(pairs, -1), turned)


def ladder_kernel(partner_ref, left_ref, right_ref, amp_ref, *rest):
    out_ref, total = rest[-2], rest[-1]
    step, last = pl.program_id(1), pl.num_programs(1) - 1
    bands, _, depth, rows, width = left_ref.shape[1:]
    vb = bands * rows
    slabs = amp_ref.shape[2] // width
    left = jnp.concatenate([left_ref[0, :, 0, g].reshape(vb, width) for g in range(depth)], axis=0)
    right = jnp.concatenate([right_ref[0, :, 0, g].reshape(vb, width) for g in range(depth)], axis=1)
    mixed = jnp.dot(left, amp_ref[0], preferred_element_type=jnp.float32).astype(jnp.bfloat16)
    wide = jnp.concatenate(
        [
            jnp.concatenate(
                [mixed[g * vb:(g + 1) * vb, s * width:(s + 1) * width] for g in range(depth)], axis=1
            )
            for s in range(slabs)
        ],
        axis=0,
    )
    part = lax.dot_general(wide, right, (((1,), (1,)), ((), ())), preferred_element_type=jnp.float32)

    @pl.when(step == 0)
    def _():
        total[...] = part if len(rest) == 2 else part + rest[0][0]

    @pl.when(step > 0)
    def _():
        total[...] += part

    @pl.when(step == last)
    def _():
        out_ref[0] = total[...].astype(out_ref.dtype)


def ladder_sums(blocks, amps, partner, before, kind):
    groups, bands, per_group, g_count, rows, width = blocks.shape
    pairs = per_group * groups
    vb = bands * rows
    depth = math.gcd(g_count, 8)
    slabs = amps.shape[2] // width

    def left_map(r, s, partner_ref):
        return (r // per_group, 0, lax.rem(r, per_group), s, 0, 0)

    def right_map(r, s, partner_ref):
        q = partner_ref[r]
        return (q // per_group, 0, lax.rem(q, per_group), s, 0, 0)

    spec = (1, bands, 1, depth, rows, width)
    sum_spec = pl.BlockSpec((1, slabs * vb, vb), lambda r, s, p: (r, 0, 0))
    return pl.pallas_call(
        ladder_kernel,
        grid_spec=pltpu.PrefetchScalarGridSpec(
            num_scalar_prefetch=1,
            grid=(pairs, g_count // depth),
            in_specs=[
                pl.BlockSpec(spec, left_map),
                pl.BlockSpec(spec, right_map),
                pl.BlockSpec((1,) + amps.shape[1:], lambda r, s, p: (r, 0, 0)),
            ] + [sum_spec] * len(before),
            out_specs=sum_spec,
            scratch_shapes=[pltpu.VMEM((slabs * vb, vb), jnp.float32)],
        ),
        out_shape=jax.ShapeDtypeStruct((pairs, slabs * vb, vb), kind),
        cost_estimate=pl.CostEstimate(
            flops=4 * pairs * g_count * vb * vb * vb * slabs, bytes_accessed=4 * blocks.size, transcendentals=0
        ),
        name="ladder",
    )(partner, blocks, blocks, amps, *before)


def shards(group_count, band_count, densities, amplitudes, partner, qtable, grid_map, coulomb):
    my_group = lax.axis_index("kgrp")
    per_group, rows, width, g_all = densities.shape
    slabs = amplitudes.shape[1]
    vb = rows * band_count
    devices = group_count * band_count
    g_shard = g_all // devices
    own_ids = my_group * per_group + jnp.arange(per_group, dtype=jnp.int32)
    transfers = jnp.take(qtable, own_ids)
    positions = jnp.take(grid_map, transfers, axis=0).reshape(per_group, devices, g_shard)
    factors = jnp.take(coulomb, transfers, axis=0).reshape(per_group, devices, g_shard)
    turned = jnp.transpose(densities, (0, 3, 1, 2))
    amps = lax.all_gather(amplitudes, "kgrp", axis=0, tiled=True)
    amps = jnp.transpose(amps, (0, 2, 1, 3)).reshape(-1, width, slabs * width)

    unit = sum(CUTS)
    counts = [g_shard * cut // unit for cut in CUTS] if g_shard % unit == 0 else [g_shard]
    picked, start = [], 0
    for count in counts:
        span = slice(start, start + count)
        start += count
        picked.append(pick_rows(turned, positions[:, :, span], factors[:, :, span]))
    before, moved = (), []

    def add_sums(at):
        kind = jnp.bfloat16 if at == len(counts) - 1 else jnp.float32
        return (ladder_sums(moved[at], amps, partner, before, kind),)

    for at, chunk in enumerate(picked):
        if at > 1:
            before = add_sums(at - 2)
            chunk, *before = lax.optimization_barrier((chunk, *before))
        chunk = lax.all_to_all(chunk, ("kgrp", "band"), split_axis=0, concat_axis=0, tiled=True)
        moved.append(chunk.reshape(group_count, band_count, per_group, counts[at], rows, width))
    for at in range(max(len(counts) - 2, 0), len(counts)):
        before = add_sums(at)

    sums = before[0].reshape(group_count, per_group, slabs, band_count, rows, vb)
    sums = jnp.transpose(sums, (0, 3, 1, 2, 4, 5)).reshape(devices, per_group, slabs, rows, vb)
    sums = lax.all_to_all(sums, ("kgrp", "band"), split_axis=0, concat_axis=0, tiled=True)
    summed = jnp.sum(sums.astype(jnp.float32), axis=0) * (1.0 / math.sqrt(g_all))
    return jnp.transpose(summed, (2, 0, 1, 3)).astype(jnp.bfloat16)


def solution(mesh):
    in_specs = (P("kgrp", "band", None, None), P("kgrp", None, None, None), P(), P(), P(), P())
    out_specs = P("band", "kgrp", None, None)
    body = functools.partial(shards, mesh.shape["kgrp"], mesh.shape["band"])
    return jax.shard_map(body, mesh=mesh, in_specs=in_specs, out_specs=out_specs, check_vma=False)
```

```python
import functools
import math

import jax
import jax.numpy as jnp
from jax import lax
from jax.experimental import pallas as pl
from jax.experimental.pallas import tpu as pltpu
from jax.sharding import PartitionSpec as P

CUTS = (3, 8, 4, 1)


def turn_kernel(source_ref, out_ref):
    rows, width, count = source_ref.shape[1:]
    flat = source_ref[0].reshape(rows * width, count)
    out_ref[0] = flat.T.reshape(count, rows, width)


def turn(densities, pair):
    _, rows, width, g_all = densities.shape
    count = math.gcd(g_all, 256)
    moved = rows * width * g_all
    return pl.pallas_call(
        turn_kernel,
        grid=(g_all // count,),
        in_specs=[pl.BlockSpec((1, rows, width, count), lambda g: (pair, 0, 0, g))],
        out_specs=pl.BlockSpec((1, count, rows, width), lambda g: (0, g, 0, 0)),
        out_shape=jax.ShapeDtypeStruct((1, g_all, rows, width), densities.dtype),
        cost_estimate=pl.CostEstimate(flops=moved, bytes_accessed=4 * moved, transcendentals=0),
        name="turn",
    )(densities)


def pick_kernel(index_ref, factor_ref, *refs):
    *source_refs, out_ref = refs
    devices, _, depth = out_ref.shape[:3]

    def one_pair(pair, source_ref):
        def one(i, carry):
            d, g = i // depth, lax.rem(i, depth)
            row = source_ref[0, index_ref[pair, i]].astype(jnp.float32) * factor_ref[pair, i]
            out_ref[d, 0, g] = row.astype(out_ref.dtype)
            return carry

        lax.fori_loop(0, devices * depth, one, 0, unroll=8)

    for pair, source_ref in enumerate(source_refs):
        pl.when(pl.program_id(0) == pair)(functools.partial(one_pair, pair, source_ref))


def pick_rows(sources, index, factors):
    pairs = len(sources)
    _, g_all, rows, width = sources[0].shape
    devices, depth = index.shape[1:]
    moved = pairs * devices * depth * rows * width
    return pl.pallas_call(
        pick_kernel,
        grid_spec=pltpu.PrefetchScalarGridSpec(
            num_scalar_prefetch=2,
            grid=(pairs,),
            in_specs=[
                pl.BlockSpec(
                    (1, g_all, rows, width), lambda p, i, f: (0, 0, 0, 0), pipeline_mode=pl.Buffered(1)
                )
            ] * pairs,
            out_specs=pl.BlockSpec((devices, 1, depth, rows, width), lambda p, i, f: (0, p, 0, 0, 0)),
        ),
        out_shape=jax.ShapeDtypeStruct((devices, pairs, depth, rows, width), sources[0].dtype),
        cost_estimate=pl.CostEstimate(
            flops=moved, bytes_accessed=2 * pairs * sources[0].size + 2 * moved, transcendentals=0
        ),
        compiler_params=pltpu.CompilerParams(vmem_limit_bytes=62 * 1024 * 1024),
        name="pick_rows",
    )(index.reshape(pairs, -1), factors.reshape(pairs, -1), *sources)


def ladder_kernel(partner_ref, slot_ref, left_ref, right_ref, amp_ref, *rest):
    out_ref, total = rest[-2], rest[-1]
    step, last = pl.program_id(1), pl.num_programs(1) - 1
    bands, _, depth, rows, width = left_ref.shape[1:]
    vb = bands * rows
    slabs = amp_ref.shape[2] // width
    left = jnp.concatenate([left_ref[0, :, 0, g].reshape(vb, width) for g in range(depth)], axis=0)
    right = jnp.concatenate([right_ref[0, :, 0, g].reshape(vb, width) for g in range(depth)], axis=1)
    mixed = jnp.dot(left, amp_ref[0], preferred_element_type=jnp.float32).astype(jnp.bfloat16)
    wide = jnp.concatenate(
        [
            jnp.concatenate(
                [mixed[g * vb:(g + 1) * vb, s * width:(s + 1) * width] for g in range(depth)], axis=1
            )
            for s in range(slabs)
        ],
        axis=0,
    )
    part = lax.dot_general(wide, right, (((1,), (1,)), ((), ())), preferred_element_type=jnp.float32)

    @pl.when(step == 0)
    def _():
        total[...] = part if len(rest) == 2 else part + rest[0][0]

    @pl.when(step > 0)
    def _():
        total[...] += part

    @pl.when(step == last)
    def _():
        out_ref[0] = total[...].astype(out_ref.dtype)


def ladder_sums(blocks, amps, partner, slots, before, kind):
    groups, bands, per_group, g_count, rows, width = blocks.shape
    pairs = per_group * groups
    vb = bands * rows
    depth = math.gcd(g_count, 8)
    slabs = amps.shape[2] // width

    def left_map(r, s, partner_ref, slot_ref):
        return (r // per_group, 0, lax.rem(r, per_group), s, 0, 0)

    def right_map(r, s, partner_ref, slot_ref):
        q = partner_ref[r]
        return (q // per_group, 0, lax.rem(q, per_group), s, 0, 0)

    def amp_map(r, s, partner_ref, slot_ref):
        return (slot_ref[r // per_group] * per_group + lax.rem(r, per_group), 0, 0)

    spec = (1, bands, 1, depth, rows, width)
    sum_spec = pl.BlockSpec((1, slabs * vb, vb), lambda r, s, p, q: (r, 0, 0))
    return pl.pallas_call(
        ladder_kernel,
        grid_spec=pltpu.PrefetchScalarGridSpec(
            num_scalar_prefetch=2,
            grid=(pairs, g_count // depth),
            in_specs=[
                pl.BlockSpec(spec, left_map),
                pl.BlockSpec(spec, right_map),
                pl.BlockSpec((1,) + amps.shape[1:], amp_map),
            ] + [sum_spec] * len(before),
            out_specs=sum_spec,
            scratch_shapes=[pltpu.VMEM((slabs * vb, vb), jnp.float32)],
        ),
        out_shape=jax.ShapeDtypeStruct((pairs, slabs * vb, vb), kind),
        cost_estimate=pl.CostEstimate(
            flops=4 * pairs * g_count * vb * vb * vb * slabs, bytes_accessed=4 * blocks.size, transcendentals=0
        ),
        name="ladder",
    )(partner, slots, blocks, blocks, amps, *before)


def shards(group_count, band_count, densities, amplitudes, partner, qtable, grid_map, coulomb):
    my_group = lax.axis_index("kgrp")
    per_group, rows, width, g_all = densities.shape
    slabs = amplitudes.shape[1]
    vb = rows * band_count
    devices = group_count * band_count
    g_shard = g_all // devices
    own_ids = my_group * per_group + jnp.arange(per_group, dtype=jnp.int32)
    transfers = jnp.take(qtable, own_ids)
    positions = jnp.take(grid_map, transfers, axis=0).reshape(per_group, devices, g_shard)
    factors = jnp.take(coulomb, transfers, axis=0).reshape(per_group, devices, g_shard)
    held = jnp.transpose(amplitudes, (0, 2, 1, 3)).reshape(per_group, width, slabs * width)
    arrived = [held]
    for shift in range(1, group_count):
        ring = [(source, (source + shift) % group_count) for source in range(group_count)]
        arrived.append(lax.ppermute(held, "kgrp", ring))
    amps = jnp.concatenate(arrived, axis=0)
    slots = lax.rem(my_group - jnp.arange(group_count, dtype=jnp.int32) + group_count, group_count)

    unit = sum(CUTS)
    counts = [g_shard * cut // unit for cut in CUTS] if g_shard % unit == 0 else [g_shard]
    starts = [sum(counts[:at]) for at in range(len(counts))]

    def exchange(chunk):
        return lax.all_to_all(chunk, ("kgrp", "band"), split_axis=0, concat_axis=0, tiled=True)

    def pick(at, first, count):
        span = slice(starts[at], starts[at] + counts[at])
        own = slice(first, first + count)
        return pick_rows(turned[own], positions[own, :, span], factors[own, :, span])

    turned, firsts, source = [], [], densities
    for p in range(per_group):
        turned.append(turn(source, p))
        chunk = pick(0, p, 1)
        chunk, source = lax.optimization_barrier((chunk, source))
        firsts.append(exchange(chunk))
    tables = [jnp.concatenate(firsts, axis=1)]

    before = ()

    def add_sums(at):
        kind = jnp.bfloat16 if at == len(counts) - 1 else jnp.float32
        blocks = tables[at].reshape(group_count, band_count, per_group, counts[at], rows, width)
        return (ladder_sums(blocks, amps, partner, slots, before, kind),)

    for at in range(1, len(counts)):
        chunk = pick(at, 0, per_group)
        if at > 1:
            before = add_sums(at - 2)
            chunk, *before = lax.optimization_barrier((chunk, *before))
        tables.append(exchange(chunk))
    for at in range(max(len(counts) - 2, 0), len(counts)):
        before = add_sums(at)

    sums = before[0].reshape(group_count, per_group, slabs, band_count, rows, vb)
    sums = jnp.transpose(sums, (0, 3, 1, 2, 4, 5)).reshape(devices, per_group, slabs, rows, vb)
    sums = lax.all_to_all(sums, ("kgrp", "band"), split_axis=0, concat_axis=0, tiled=True)
    summed = jnp.sum(sums.astype(jnp.float32), axis=0) * (1.0 / math.sqrt(g_all))
    return jnp.transpose(summed, (2, 0, 1, 3)).astype(jnp.bfloat16)


def solution(mesh):
    in_specs = (P("kgrp", "band", None, None), P("kgrp", None, None, None), P(), P(), P(), P())
    out_specs = P("band", "kgrp", None, None)
    body = functools.partial(shards, mesh.shape["kgrp"], mesh.shape["band"])
    return jax.shard_map(body, mesh=mesh, in_specs=in_specs, out_specs=out_specs, check_vma=False)
```
